32 devices in a mesh: sec: 4 (over y, x), term: 8 (over z, core).
Axes of the slice: x: 2, y: 2, z: 4, core: 2. Of those that a mesh axis runs over, the one named last changes fastest.
Arguments:
- theta: bfloat16 [4, 896, 896], P('sec', 'term'), may hold values from -6 to 6
- left_env: bfloat16 [16, 4, 896, 896], P('term', 'sec'), may hold values from -2 to 2
- right_env: bfloat16 [16, 4, 896, 896], P('term', 'sec'), may hold values from -2 to 2
- term_shift: int32 [16], P('term'), may hold values from -1 to 1
- term_on: int32 [16, 4], P('term', 'sec'), may hold values 0 or 1
- block_rows: int32 [4], P('sec'), may hold values from 224 to 896
- block_cols: int32 [4], P('sec'), may hold values from 224 to 896
Outputs:
- basis_last: float32 [4, 896, 896], P('sec', 'term')
- alphas: float32 [2], replicated
- betas: float32 [2], replicated
The draws below stay inside these ranges and needn't reach their ends.
All inputs are finite; a program needn't handle non-finite values. No bound on the sum of `term_on` on one device may be relied on, other than what follows from the above.
Results may differ from the reference program's by a relative error of at most 0.0037.
Values may be sent and summed in bfloat16 or wider, within the bound.
No kernel may reach another device: no remote copies, remote signals or barrier semaphores. Data moves between devices by JAX's collectives and lax.ppermute only.
A program may use at most 64 MiB of HBM per device.

```python
import math
import jax
import jax.numpy as jnp
from jax import lax

B = 896
ITERS = 2
SECTORS = 4
TERMS = 16


SHARED_WEIGHT = 0.7


SEPARATE_WEIGHT = 0.7


DIAGONAL_WEIGHT = 0.5


def environment_draw(key, first, second):
    shared_key = jax.random.fold_in(key, first)
    separate_key = jax.random.fold_in(key, second)
    scale = 1.0 / math.sqrt(B)
    shared_part = jnp.clip(jax.random.normal(shared_key, (SECTORS, B, B), jnp.float32), -6.0, 6.0)
    separate_part = jnp.clip(jax.random.normal(separate_key, (TERMS, SECTORS, B, B), jnp.float32), -6.0, 6.0)
    identity = jnp.eye(B, dtype=jnp.float32)
    total = (SHARED_WEIGHT * shared_part[None] + SEPARATE_WEIGHT * separate_part) * scale + DIAGONAL_WEIGHT * identity[None, None]
    return total.astype(jnp.bfloat16)


def draw_left_env(key, part):
    return environment_draw(key, 11, 12)


def draw_right_env(key, part):
    return environment_draw(key, 21, 22)


def set_ends(array, rng, least, top_value):
    place = [jax.random.randint(jax.random.fold_in(rng, axis), (), 0, length) for axis, length in enumerate(array.shape)]
    widest = array.shape.index(max(array.shape))
    beside = place[:widest] + [(place[widest] + 1) % array.shape[widest]] + place[widest + 1:]
    return array.at[tuple(place)].set(least).at[tuple(beside)].set(top_value)


def block_scale(rng, dims, pieces, smallest, top_value):
    def one(axis_at, parts):
        heights = jax.random.uniform(jax.random.fold_in(jax.random.fold_in(rng, 6), axis_at), (parts,), jnp.float32, smallest / len(pieces), top_value / len(pieces))
        return jnp.repeat(jnp.exp(heights), dims[axis_at] // parts).reshape((-1,) + (1,) * (len(dims) - axis_at - 1))

    loudness = one(*pieces[0])
    for cut in pieces[1:]:
        loudness = loudness * one(*cut)
    return loudness


def centred(own_key, extent, scale, reach, shards=(), kind=jnp.bfloat16):
    loudness = block_scale(own_key, extent, shards, -0.22, 0.18) if shards else 1.0
    values = jax.random.normal(own_key, extent, jnp.float32) * scale * loudness
    return jnp.minimum(jnp.maximum(values, -reach), reach).astype(kind)


def setup_inputs(seed: int = 0) -> dict:
    splits = jax.random.split(jax.random.key(seed), 8)
    theta = centred(splits[0], (SECTORS, B, B), 1.0, 6.0, ((0, 4), (1, 8)))
    left_env = draw_left_env(jax.random.fold_in(splits[7], 71), 0)
    right_env = draw_right_env(jax.random.fold_in(splits[7], 71), 0)
    term_shift = set_ends(jax.random.randint(splits[3], (TERMS,), -1, 2), jax.random.fold_in(splits[3], 1), -1, 1).astype(jnp.int32)
    term_on = set_ends((jax.random.randint(splits[4], (TERMS, SECTORS), 0, 4) < 3).astype(jnp.int32), jax.random.fold_in(splits[4], 1), 0, 1)
    block_rows = set_ends(jax.random.randint(splits[5], (SECTORS,), B // 4, B + 1), jax.random.fold_in(splits[5], 1), B // 4, B).astype(jnp.int32)
    block_cols = set_ends(jax.random.randint(splits[6], (SECTORS,), B // 4, B + 1), jax.random.fold_in(splits[6], 1), B // 4, B).astype(jnp.int32)
    return dict(theta=theta, left_env=left_env, right_env=right_env, term_shift=term_shift, term_on=term_on, block_rows=block_rows, block_cols=block_cols)


EPS = 1e-06

def block_mask(block_rows, block_cols):
    index_line = jnp.arange(B, dtype=jnp.int32)
    inside_rows = index_line[None, :] < block_rows[:, None]
    inside_cols = index_line[None, :] < block_cols[:, None]
    return (inside_rows[:, :, None] & inside_cols[:, None, :]).astype(jnp.float32)

def apply_operator(vector_bf, left_env, right_env, term_shift, term_on, mask):
    count = vector_bf.shape[0]
    zero_block = jnp.zeros((1, B, B), jnp.bfloat16)
    padded = jnp.concatenate([zero_block, vector_bf, zero_block], axis=0)

    def one_term(total, inputs):
        left_term, right_term, shift_value, on_value = inputs
        sources = lax.dynamic_slice_in_dim(padded, (1 + shift_value).astype(jnp.int32), count, 0)
        product = jnp.einsum('sik,skj->sij', left_term.astype(jnp.float32), sources.astype(jnp.float32)).astype(jnp.bfloat16)
        result = jnp.einsum('sij,sjk->sik', product.astype(jnp.float32), right_term.astype(jnp.float32))
        return (total + on_value.astype(jnp.float32)[:, None, None] * result, None)
    total, _ = lax.scan(one_term, jnp.zeros((count, B, B), jnp.float32), (left_env, right_env, term_shift, term_on))
    return mask * total

def reference(theta, left_env, right_env, term_shift, term_on, block_rows, block_cols):
    mask = block_mask(block_rows, block_cols)
    start = mask * theta.astype(jnp.float32)
    vector = start / jnp.sqrt(jnp.sum(start * start) + EPS)
    previous = jnp.zeros_like(vector)
    beta_prev = jnp.float32(0.0)
    alpha_list = []
    beta_list = []
    for step in range(ITERS):
        image = apply_operator(vector.astype(jnp.bfloat16), left_env, right_env, term_shift, term_on, mask)
        alpha = jnp.sum(vector * image)
        residual = image - alpha * vector - beta_prev * previous
        beta = jnp.sqrt(jnp.sum(residual * residual) + EPS)
        previous = vector
        vector = residual / beta
        beta_prev = beta
        alpha_list.append(alpha)
        beta_list.append(beta)
    return (vector, jnp.stack(alpha_list), jnp.stack(beta_list))
```

```python
import functools

import jax
import jax.numpy as jnp
from jax import lax
from jax.experimental import pallas as pl
from jax.experimental.pallas import tpu as pltpu
from jax.sharding import PartitionSpec as P

ITERS = 2


EPS = 1e-06

SCALE = 2.0**-10


def along_term(x, partner, count):
    return lax.ppermute(x, "term", [(i, partner(i)) for i in range(count)])


def pair_exchange(x, count):
    return lax.ppermute(x, "sec", [(i, i ^ 1) for i in range(count) if (i ^ 1) < count])


def pair_forward(x, count):
    pairs = [(i, i + 2) for i in range(0, count, 2) if i + 2 < count]
    pairs += [(i, i - 2) for i in range(1, count, 2) if i >= 2]
    return lax.ppermute(x, "sec", pairs)


def gather_pieces(shard, sec_count, term_count):
    chips = term_count // 2
    own = {0: shard}
    order = sorted(range(1, chips), key=lambda i: (bin(i).count("1"), i))
    for i in order:
        bit = i & -i
        own[i] = along_term(own[i ^ bit], lambda t, b=bit: t ^ (2 * b), term_count)
    pair = {i: pair_exchange(own[i], sec_count) for i in range(chips)}
    beyond = {i: pair_forward(pair[i], sec_count) for i in range(chips)}
    pieces = []
    for table in (own, pair, beyond):
        for i in range(chips):
            pieces.append(table[i])
            pieces.append(along_term(table[i], lambda t: t ^ 1, term_count))
    return pieces


def apply_kernel(chips, terms, rows, scal, left, right, *refs):
    pieces = refs[: 6 * chips]
    mine, theirs, x_s, l_s, r_s, a_s, x_sem, l_sem, r_sem = refs[6 * chips :]
    width = x_s.shape[2]
    z, c = scal[2 * terms], scal[2 * terms + 1]
    block_rows, block_cols = scal[2 * terms + 2], scal[2 * terms + 3]

    def offset(i, other):
        t = jnp.bitwise_xor(z, i) * 2 + jnp.bitwise_xor(c, other)
        return pl.multiple_of(t * rows, rows)

    def piece_copy(w, source, i, other):
        return pltpu.make_async_copy(
            pieces[source * 2 * chips + 2 * i + other].at[0],
            x_s.at[w, pl.ds(offset(i, other), rows)],
            x_sem.at[w],
        )

    def l_copy(w):
        return pltpu.make_async_copy(left.at[w, 0], l_s.at[w], l_sem.at[w])

    def r_copy(w):
        return pltpu.make_async_copy(right.at[w, 0], r_s.at[pl.ds(w * width, width)], r_sem.at[w])

    for w in range(terms):
        l_copy(w).start()
        for source in range(3):

            @pl.when(scal[w] == source)
            def _():
                for i in range(chips):
                    for other in range(2):
                        piece_copy(w, source, i, other).start()

    for w in range(terms):
        r_copy(w).start()

    for w in range(terms):
        l_copy(w).wait()
        for i in range(chips):
            for other in range(2):
                piece_copy(w, 0, i, other).wait()
        on = scal[terms + w].astype(jnp.float32)
        for i in range(chips):
            band = slice(i * 2 * rows, (i + 1) * 2 * rows)
            product = jnp.dot(l_s[w, band, :], x_s[w], preferred_element_type=jnp.float32)
            a_s[band, w * width : (w + 1) * width] = (product * on).astype(jnp.bfloat16)
    for w in range(terms):
        r_copy(w).wait()
    col = lax.broadcasted_iota(jnp.int32, (2 * rows, width), 1)
    row = lax.broadcasted_iota(jnp.int32, (2 * rows, width), 0)
    for i in range(chips):
        start = pl.multiple_of(jnp.bitwise_xor(z, i) * 2 * rows, 2 * rows)
        total = jnp.dot(a_s[pl.ds(start, 2 * rows), :], r_s[...], preferred_element_type=jnp.float32)
        inside = (row + start < block_rows) & (col < block_cols)
        total = jnp.where(inside, total, 0.0)
        first = c == 0
        mine[i] = jnp.where(first, total[:rows], total[rows:])
        theirs[i] = jnp.where(first, total[rows:], total[:rows]).astype(jnp.bfloat16)


def apply_terms(scal, left_env, right_env, pieces, chips, rows):
    terms, _, width, _ = left_env.shape
    return pl.pallas_call(
        functools.partial(apply_kernel, chips, terms, rows),
        out_shape=(
            jax.ShapeDtypeStruct((chips, rows, width), jnp.float32),
            jax.ShapeDtypeStruct((chips, rows, width), jnp.bfloat16),
        ),
        in_specs=[pl.BlockSpec(memory_space=pltpu.SMEM)]
        + [pl.BlockSpec(memory_space=pl.ANY)] * (2 + len(pieces)),
        out_specs=(pl.BlockSpec(memory_space=pltpu.VMEM),) * 2,
        scratch_shapes=[
            pltpu.VMEM((terms, width, width), jnp.bfloat16),
            pltpu.VMEM((terms, width, width), jnp.bfloat16),
            pltpu.VMEM((terms * width, width), jnp.bfloat16),
            pltpu.VMEM((width, terms * width), jnp.bfloat16),
            pltpu.SemaphoreType.DMA((terms,)),
            pltpu.SemaphoreType.DMA((terms,)),
            pltpu.SemaphoreType.DMA((terms,)),
        ],
        compiler_params=pltpu.CompilerParams(vmem_limit_bytes=40 * 2**20),
        name="apply_terms",
    )(scal, left_env, right_env, *pieces)


def reduce_rows(mine, theirs, term_count):
    got = along_term(theirs, lambda t: t ^ 1, term_count)
    chips = term_count // 2
    total = mine[0] + got[0].astype(jnp.float32)
    for i in range(1, chips):
        part = (mine[i] + got[i].astype(jnp.float32)).astype(jnp.bfloat16)
        part = along_term(part, lambda t, b=i: t ^ (2 * b), term_count)
        total = total + part.astype(jnp.float32)
    return total


def sum_all(values, sec_count, term_count):
    tile = jnp.broadcast_to(jnp.stack(values)[:, None], (len(values), 128))
    tile = jnp.pad(tile, ((0, 8 - len(values)), (0, 0)))
    bit = 1
    while bit < term_count:
        tile = tile + along_term(tile, lambda t, b=bit: t ^ b, term_count)
        bit *= 2
    bit = 1
    while bit < sec_count:
        tile = tile + lax.ppermute(tile, "sec", [(i, i ^ bit) for i in range(sec_count)])
        bit *= 2
    return [tile[i, 0] for i in range(len(values))]


def on_device(theta, left_env, right_env, term_shift, term_on, block_rows, block_cols):
    rows, width = theta.shape[1:]
    sec_count, term_count = lax.axis_size("sec"), lax.axis_size("term")
    sec, term = lax.axis_index("sec"), lax.axis_index("term")
    chips = term_count // 2
    row = term * rows + lax.broadcasted_iota(jnp.int32, (1, rows, width), 1)
    col = lax.broadcasted_iota(jnp.int32, (1, rows, width), 2)
    start = jnp.where((row < block_rows[0]) & (col < block_cols[0]), theta, jnp.zeros_like(theta))
    toward_pair = 1 - 2 * (sec % 2)
    source = jnp.where(term_shift == 0, 0, jnp.where(term_shift == toward_pair, 1, 2))
    scal = jnp.concatenate(
        [source, term_on[:, 0], jnp.stack([term // 2, term % 2]), block_rows, block_cols]
    ).astype(jnp.int32)

    def apply(shard):
        pieces = gather_pieces(shard, sec_count, term_count)
        mine, theirs = apply_terms(scal, left_env, right_env, pieces, chips, rows)
        return reduce_rows(mine, theirs, term_count)

    x = start[0].astype(jnp.float32)
    y = apply(start) * SCALE
    h = apply(y.astype(jnp.bfloat16)[None])
    pairs = ((x, x), (x, y), (y, y), (x, h), (y, h), (h, h))
    xx, xy, yy, xh, yh, hh = sum_all([jnp.sum(a * b) for a, b in pairs], sec_count, term_count)
    cx = 1.0 / jnp.sqrt(xx + EPS)
    cy = cx / SCALE
    vv, vi, ii = xx * cx * cx, xy * cx * cy, yy * cy * cy
    vh, ih, hh = xh * cx * cy, yh * cy * cy, hh * cy * cy
    alpha0 = vi
    beta0 = jnp.sqrt(jnp.maximum(ii - 2.0 * alpha0 * vi + alpha0 * alpha0 * vv, 0.0) + EPS)
    inv = 1.0 / beta0
    ui = (ii - alpha0 * vi) * inv
    uh = (ih - alpha0 * vh) * inv
    uv = (vi - alpha0 * vv) * inv
    uu = (ui - alpha0 * uv) * inv
    jv = (vh - alpha0 * vi) * inv
    jj = (hh - 2.0 * alpha0 * ih + alpha0 * alpha0 * ii) * inv * inv
    alpha1 = (uh - alpha0 * ui) * inv
    square = (
        jj + alpha1 * alpha1 * uu + beta0 * beta0 * vv
        - 2.0 * alpha1 * alpha1 - 2.0 * beta0 * jv + 2.0 * alpha1 * beta0 * uv
    )
    beta1 = jnp.sqrt(jnp.maximum(square, 0.0) + EPS)
    last = 1.0 / beta1
    ch = inv * last * cy
    ci = -(alpha0 + alpha1) * inv * last * cy
    cv = (alpha1 * alpha0 * inv - beta0) * last * cx
    vector = ch * h + ci * y + cv * x
    return (vector[None], jnp.stack([alpha0, alpha1]), jnp.stack([beta0, beta1]))


def solution(mesh):
    return jax.shard_map(
        on_device,
        mesh=mesh,
        in_specs=(
            P("sec", "term", None),
            P("term", "sec", None, None),
            P("term", "sec", None, None),
            P("term"),
            P("term", "sec"),
            P("sec"),
            P("sec"),
        ),
        out_specs=(P("sec", "term", None), P(), P()),
        check_vma=False,
    )
```

```python
import functools

import jax
import jax.numpy as jnp
from jax import lax
from jax.experimental import pallas as pl
from jax.experimental.pallas import tpu as pltpu
from jax.sharding import PartitionSpec as P

ITERS = 2


EPS = 1e-06

SCALE = 2.0**-10


def along_term(x, partner, count):
    return lax.ppermute(x, "term", [(i, partner(i)) for i in range(count)])


def pair_exchange(x, count):
    return lax.ppermute(x, "sec", [(i, i ^ 1) for i in range(count) if (i ^ 1) < count])


def pair_forward(x, count):
    pairs = [(i, i + 2) for i in range(0, count, 2) if i + 2 < count]
    pairs += [(i, i - 2) for i in range(1, count, 2) if i >= 2]
    return lax.ppermute(x, "sec", pairs)


def gather_pieces(shard, beside, sec_count, term_count):
    chips = term_count // 2
    own = {0: shard}
    order = sorted(range(1, chips), key=lambda i: (bin(i).count("1"), i))
    for i in order:
        bit = i & -i
        own[i] = along_term(own[i ^ bit], lambda t, b=bit: t ^ (2 * b), term_count)
    pair, beyond = {}, {}
    held, beside = lax.optimization_barrier((own[1], beside))
    own[1] = held
    for i in range(chips):
        pair[i] = pair_exchange(own[i], sec_count)
    for i in range(chips):
        beyond[i] = pair_forward(pair[i], sec_count)
    pieces = []
    for table in (own, pair, beyond):
        for i in range(chips):
            pieces.append(table[i])
            pieces.append(along_term(table[i], lambda t: t ^ 1, term_count))
    return pieces, beside


def apply_kernel(chips, terms, rows, scal, left, right, *refs):
    pieces = refs[: 6 * chips]
    mine, theirs, x_s, l_s, r_s, a_s, l_sem, r_sem = refs[6 * chips :]
    width = x_s.shape[2]
    z, c = scal[2 * terms], scal[2 * terms + 1]
    block_rows, block_cols = scal[2 * terms + 2], scal[2 * terms + 3]

    def l_copy(w):
        return pltpu.make_async_copy(left.at[w, 0], l_s.at[w], l_sem.at[w])

    def r_copy(w):
        return pltpu.make_async_copy(right.at[w, 0], r_s.at[pl.ds(w * width, width)], r_sem.at[w])

    for w in range(terms):
        l_copy(w).start()
    for w in range(terms):
        r_copy(w).start()
    for w in range(terms):
        for source in range(3):

            @pl.when(scal[w] == source)
            def _():
                for i in range(chips):
                    for other in range(2):
                        t = jnp.bitwise_xor(z, i) * 2 + jnp.bitwise_xor(c, other)
                        piece = pieces[source * 2 * chips + 2 * i + other]
                        x_s[w, pl.ds(pl.multiple_of(t * rows, rows), rows), :] = piece[0]

    for w in range(terms):
        on = scal[terms + w].astype(jnp.float32)
        l_copy(w).wait()
        product = jnp.dot(l_s[w], x_s[w], preferred_element_type=jnp.float32)
        a_s[:, w * width : (w + 1) * width] = (product * on).astype(jnp.bfloat16)
    for w in range(terms):
        r_copy(w).wait()
    col = lax.broadcasted_iota(jnp.int32, (2 * rows, width), 1)
    row = lax.broadcasted_iota(jnp.int32, (2 * rows, width), 0)
    for i in range(chips):
        start = pl.multiple_of(jnp.bitwise_xor(z, i) * 2 * rows, 2 * rows)
        total = jnp.dot(
            a_s[pl.ds(start, 2 * rows), :], r_s[...], preferred_element_type=jnp.float32
        )
        inside = (row + start < block_rows) & (col < block_cols)
        total = jnp.where(inside, total, 0.0)
        first = c == 0
        mine[i] = jnp.where(first, total[:rows], total[rows:])
        theirs[i] = jnp.where(first, total[rows:], total[:rows]).astype(theirs.dtype)


def apply_terms(scal, left_env, right_env, pieces, rows):
    terms, _, width, _ = left_env.shape
    chips = len(pieces) // 6
    smem, hbm, vmem = (
        pl.BlockSpec(memory_space=m) for m in (pltpu.SMEM, pltpu.HBM, pltpu.VMEM)
    )
    return pl.pallas_call(
        functools.partial(apply_kernel, chips, terms, rows),
        out_shape=(
            jax.ShapeDtypeStruct((chips, rows, width), jnp.float32),
            jax.ShapeDtypeStruct((chips, rows, width), jnp.bfloat16),
        ),
        in_specs=[smem, hbm, hbm] + [vmem] * len(pieces),
        out_specs=(vmem, vmem),
        scratch_shapes=[
            pltpu.VMEM((terms, width, width), jnp.bfloat16),
            pltpu.VMEM((terms, width, width), jnp.bfloat16),
            pltpu.VMEM((terms * width, width), jnp.bfloat16),
            pltpu.VMEM((width, terms * width), jnp.bfloat16),
            pltpu.SemaphoreType.DMA((terms,)),
            pltpu.SemaphoreType.DMA((terms,)),
        ],
        compiler_params=pltpu.CompilerParams(vmem_limit_bytes=46 * 2**20),
        name="apply_terms",
    )(scal, left_env, right_env, *pieces)


def reduce_parts(mine, theirs, term_count):
    other = along_term(theirs, lambda t: t ^ 1, term_count)
    totals = [mine[i] + other[i].astype(jnp.float32) for i in range(term_count // 2)]
    parts = [
        along_term(totals[i].astype(jnp.bfloat16), lambda t, b=i: t ^ (2 * b), term_count)
        for i in range(1, term_count // 2)
    ]
    return totals[0], parts


def all_sum(tile, sec_count, term_count):
    bit = 1
    while bit < term_count:
        tile = tile + along_term(tile, lambda t, b=bit: t ^ b, term_count)
        bit *= 2
    bit = 1
    while bit < sec_count:
        tile = tile + lax.ppermute(tile, "sec", [(i, i ^ bit) for i in range(sec_count)])
        bit *= 2
    return tile


def lane_sums(tile, products):
    for k, (a, b) in products.items():
        line = jnp.sum(a * b, axis=0, keepdims=True)
        tile[k : k + 1, :] = sum(line[:, j : j + 128] for j in range(0, line.shape[1], 128))


def first_gram_kernel(x_ref, y_ref, tile):
    x, y = x_ref[0].astype(jnp.float32), y_ref[...]
    tile[...] = jnp.zeros_like(tile)
    lane_sums(tile, {0: (x, x), 1: (x, y), 2: (y, y)})


def gram_kernel(before, x_ref, y_ref, own, *refs):
    h_ref, tile = refs[-2:]
    h = own[...]
    for part in refs[:-2]:
        h = h + part[...].astype(jnp.float32)
    h_ref[...] = h
    x, y = x_ref[0].astype(jnp.float32), y_ref[...]
    tile[...] = before[...]
    lane_sums(tile, {3: (x, h), 4: (y, h), 5: (h, h)})


def finish_kernel(tile, x_ref, y_ref, h_ref, vector, alphas, betas):
    sums = jnp.sum(tile[...], axis=1, keepdims=True)
    xx, xy, yy, xh, yh, hh = (sums[k : k + 1, :] for k in range(6))
    cx = 1.0 / jnp.sqrt(xx + EPS)
    cy = cx / SCALE
    vv, vi, ii = xx * cx * cx, xy * cx * cy, yy * cy * cy
    vh, ih, hh = xh * cx * cy, yh * cy * cy, hh * cy * cy
    alpha0 = vi
    square0 = ii - 2.0 * alpha0 * vi + alpha0 * alpha0 * vv
    beta0 = jnp.sqrt(jnp.maximum(square0, 0.0) + EPS)
    inv = 1.0 / beta0
    ui = (ii - alpha0 * vi) * inv
    uh = (ih - alpha0 * vh) * inv
    uv = (vi - alpha0 * vv) * inv
    uu = (ui - alpha0 * uv) * inv
    jv = (vh - alpha0 * vi) * inv
    jj = (hh - 2.0 * alpha0 * ih + alpha0 * alpha0 * ii) * inv * inv
    alpha1 = (uh - alpha0 * ui) * inv
    square1 = (
        jj + alpha1 * alpha1 * uu + beta0 * beta0 * vv
        - 2.0 * alpha1 * alpha1 - 2.0 * beta0 * jv + 2.0 * alpha1 * beta0 * uv
    )
    beta1 = jnp.sqrt(jnp.maximum(square1, 0.0) + EPS)
    last = 1.0 / beta1
    ch = inv * last * cy
    ci = -(alpha0 + alpha1) * inv * last * cy
    cv = (alpha1 * alpha0 * inv - beta0) * last * cx
    vector[0] = ch * h_ref[...] + ci * y_ref[...] + cv * x_ref[0].astype(jnp.float32)
    alphas[0], alphas[1] = alpha0[0, 0], alpha1[0, 0]
    betas[0], betas[1] = beta0[0, 0], beta1[0, 0]


def on_device(theta, left_env, right_env, term_shift, term_on, block_rows, block_cols):
    rows, width = theta.shape[1:]
    sec_count, term_count = lax.axis_size("sec"), lax.axis_size("term")
    sec, term = lax.axis_index("sec"), lax.axis_index("term")
    row = term * rows + lax.broadcasted_iota(jnp.int32, (1, rows, width), 1)
    col = lax.broadcasted_iota(jnp.int32, (1, rows, width), 2)
    start = jnp.where((row < block_rows[0]) & (col < block_cols[0]), theta, jnp.zeros_like(theta))
    toward_pair = 1 - 2 * (sec % 2)
    source = jnp.where(term_shift == 0, 0, jnp.where(term_shift == toward_pair, 1, 2))
    scal = jnp.concatenate(
        [source, term_on[:, 0], jnp.stack([term // 2, term % 2]), block_rows, block_cols]
    ).astype(jnp.int32)

    vmem, smem = (pl.BlockSpec(memory_space=m) for m in (pltpu.VMEM, pltpu.SMEM))
    small = pltpu.CompilerParams(vmem_limit_bytes=8 * 2**20)
    block = jax.ShapeDtypeStruct((rows, width), jnp.float32)
    tile = jax.ShapeDtypeStruct((8, 128), jnp.float32)
    pair = jax.ShapeDtypeStruct((2,), jnp.float32)

    pieces, scal = gather_pieces(start, scal, sec_count, term_count)
    mine, theirs = apply_terms(scal, left_env, right_env, pieces, rows)
    own, got = reduce_parts(mine, theirs, term_count)
    y = (own + sum(part.astype(jnp.float32) for part in got)) * SCALE
    sums = pl.pallas_call(
        first_gram_kernel, out_shape=tile, in_specs=[vmem] * 2, out_specs=vmem,
        compiler_params=small, name="first_gram",
    )(start, y)
    shard = y.astype(jnp.bfloat16)[None]
    pieces, sums = gather_pieces(shard, sums, sec_count, term_count)
    mine, theirs = apply_terms(scal, left_env, right_env, pieces, rows)
    own, got = reduce_parts(mine, theirs, term_count)
    h, sums = pl.pallas_call(
        gram_kernel,
        out_shape=(block, tile),
        in_specs=[vmem] * (4 + len(got)),
        out_specs=(vmem, vmem),
        compiler_params=small,
        name="gram",
    )(sums, start, y, own, *got)
    sums = all_sum(sums, sec_count, term_count)
    vector, alphas, betas = pl.pallas_call(
        finish_kernel,
        out_shape=(jax.ShapeDtypeStruct((1, rows, width), jnp.float32), pair, pair),
        in_specs=[vmem] * 4,
        out_specs=(vmem, smem, smem),
        compiler_params=small,
        name="finish",
    )(sums, start, y, h)
    return (vector, alphas, betas)


def solution(mesh):
    return jax.shard_map(
        on_device,
        mesh=mesh,
        in_specs=(
            P("sec", "term", None),
            P("term", "sec", None, None),
            P("term", "sec", None, None),
            P("term"),
            P("term", "sec"),
            P("sec"),
            P("sec"),
        ),
        out_specs=(P("sec", "term", None), P(), P()),
        check_vma=False,
    )
```

```python
import functools

import jax
import jax.numpy as jnp
from jax import lax
from jax.experimental import pallas as pl
from jax.experimental.pallas import tpu as pltpu
from jax.sharding import PartitionSpec as P

ITERS = 2


EPS = 1e-06

SCALE = 2.0**-10


def along_term(x, partner, count):
    return lax.ppermute(x, "term", [(i, partner(i)) for i in range(count)])


def pair_exchange(x, count):
    return lax.ppermute(x, "sec", [(i, i ^ 1) for i in range(count) if (i ^ 1) < count])


def pair_forward(x, count):
    pairs = [(i, i + 2) for i in range(0, count, 2) if i + 2 < count]
    pairs += [(i, i - 2) for i in range(1, count, 2) if i >= 2]
    return lax.ppermute(x, "sec", pairs)


def across_pairs(x, count):
    pairs = [(i, i + 1) for i in range(1, count - 1, 2)]
    return lax.ppermute(x, "sec", pairs + [(j, i) for i, j in pairs])


def after(x, *others):
    return lax.optimization_barrier((x,) + others)[0]


def gather_pieces(shard, beside, sec_count, term_count):
    chips = term_count // 2

    def hop(x, bit):
        return along_term(x, lambda t: t ^ (2 * bit), term_count)

    own = {0: shard}
    for i in sorted(range(1, chips), key=lambda i: (bin(i).count("1"), i)):
        own[i] = hop(own[i ^ (i & -i)], i & -i)
    own[1], beside = lax.optimization_barrier((own[1], beside))
    last = chips - 1
    pair = {i: pair_exchange(own[i], sec_count) for i in range(last)}
    pair[last] = hop(pair[last ^ 1], 1)
    beyond = {}
    for i in range(last):
        if i >= chips // 2:
            beyond[i] = pair_forward(pair[i], sec_count)
        else:
            beyond[i] = across_pairs(after(own[i], own[last]) if i else own[i], sec_count)
    beyond[last] = hop(beyond[last ^ 1], 1)
    pieces = []
    for table in (own, pair, beyond):
        for i in range(chips):
            pieces.append(table[i])
            pieces.append(along_term(table[i], lambda t: t ^ 1, term_count))
    return pieces, beside


def apply_kernel(chips, terms, rows, scal, left, right, *refs):
    pieces = refs[: 6 * chips]
    mine, theirs, x_s, l_s, r_s, a_s, l_sem, r_sem = refs[6 * chips :]
    width = x_s.shape[2]
    z, c = scal[2 * terms], scal[2 * terms + 1]
    block_rows, block_cols = scal[2 * terms + 2], scal[2 * terms + 3]

    def l_copy(w):
        return pltpu.make_async_copy(left.at[w, 0], l_s.at[w], l_sem.at[w])

    def r_copy(w):
        return pltpu.make_async_copy(right.at[w, 0], r_s.at[pl.ds(w * width, width)], r_sem.at[w])

    for w in range(terms):
        l_copy(w).start()
    for w in range(terms):
        r_copy(w).start()
    for w in range(terms):
        for source in range(3):

            @pl.when(scal[w] == source)
            def _():
                for i in range(chips):
                    for other in range(2):
                        t = jnp.bitwise_xor(z, i) * 2 + jnp.bitwise_xor(c, other)
                        piece = pieces[source * 2 * chips + 2 * i + other]
                        x_s[w, pl.ds(pl.multiple_of(t * rows, rows), rows), :] = piece[0]

    for w in range(terms):
        on = scal[terms + w].astype(jnp.float32)
        l_copy(w).wait()
        product = jnp.dot(l_s[w], x_s[w], preferred_element_type=jnp.float32)
        a_s[:, w * width : (w + 1) * width] = (product * on).astype(jnp.bfloat16)
    for w in range(terms):
        r_copy(w).wait()
    col = lax.broadcasted_iota(jnp.int32, (2 * rows, width), 1)
    row = lax.broadcasted_iota(jnp.int32, (2 * rows, width), 0)
    for i in range(chips):
        start = pl.multiple_of(jnp.bitwise_xor(z, i) * 2 * rows, 2 * rows)
        total = jnp.dot(
            a_s[pl.ds(start, 2 * rows), :], r_s[...], preferred_element_type=jnp.float32
        )
        inside = (row + start < block_rows) & (col < block_cols)
        total = jnp.where(inside, total, 0.0)
        first = c == 0
        mine[i] = jnp.where(first, total[:rows], total[rows:])
        theirs[i] = jnp.where(first, total[rows:], total[:rows]).astype(theirs.dtype)


def apply_terms(scal, left_env, right_env, pieces, rows):
    terms, _, width, _ = left_env.shape
    chips = len(pieces) // 6
    smem, hbm, vmem = (
        pl.BlockSpec(memory_space=m) for m in (pltpu.SMEM, pltpu.HBM, pltpu.VMEM)
    )
    return pl.pallas_call(
        functools.partial(apply_kernel, chips, terms, rows),
        out_shape=(
            jax.ShapeDtypeStruct((chips, rows, width), jnp.float32),
            jax.ShapeDtypeStruct((chips, rows, width), jnp.bfloat16),
        ),
        in_specs=[smem, hbm, hbm] + [vmem] * len(pieces),
        out_specs=(vmem, vmem),
        scratch_shapes=[
            pltpu.VMEM((terms, width, width), jnp.bfloat16),
            pltpu.VMEM((terms, width, width), jnp.bfloat16),
            pltpu.VMEM((terms * width, width), jnp.bfloat16),
            pltpu.VMEM((width, terms * width), jnp.bfloat16),
            pltpu.SemaphoreType.DMA((terms,)),
            pltpu.SemaphoreType.DMA((terms,)),
        ],
        compiler_params=pltpu.CompilerParams(vmem_limit_bytes=46 * 2**20),
        name="apply_terms",
    )(scal, left_env, right_env, *pieces)


def reduce_parts(mine, theirs, term_count):
    other = along_term(theirs, lambda t: t ^ 1, term_count)
    totals = [mine[i] + other[i].astype(jnp.float32) for i in range(term_count // 2)]
    parts = [
        along_term(totals[i].astype(jnp.bfloat16), lambda t, b=i: t ^ (2 * b), term_count)
        for i in range(1, term_count // 2)
    ]
    return totals[0], parts


def everyones(tile, count):
    return lax.all_to_all(jnp.broadcast_to(tile, (count,) + tile.shape), ("sec", "term"), 0, 0)


def lane_sums(tile, products):
    for k, (a, b) in products.items():
        line = jnp.sum(a * b, axis=0, keepdims=True)
        tile[k : k + 1, :] = sum(line[:, j : j + 128] for j in range(0, line.shape[1], 128))


def image_kernel(x_ref, own, *refs):
    y_ref, shard, tile = refs[-3:]
    y = own[...]
    for part in refs[:-3]:
        y = y + part[...].astype(jnp.float32)
    y = y * SCALE
    y_ref[...] = y
    shard[0] = y.astype(jnp.bfloat16)
    x = x_ref[0].astype(jnp.float32)
    tile[...] = jnp.zeros_like(tile)
    lane_sums(tile, {0: (x, x), 1: (x, y), 2: (y, y)})


def gram_kernel(before, x_ref, y_ref, own, *refs):
    h_ref, tile = refs[-2:]
    h = own[...]
    for part in refs[:-2]:
        h = h + part[...].astype(jnp.float32)
    h_ref[...] = h
    x, y = x_ref[0].astype(jnp.float32), y_ref[...]
    tile[...] = before[...]
    lane_sums(tile, {3: (x, h), 4: (y, h), 5: (h, h)})


def finish_kernel(tiles, x_ref, y_ref, h_ref, vector, alphas, betas):
    sums = jnp.sum(jnp.sum(tiles[...], axis=0), axis=1, keepdims=True)
    xx, xy, yy, xh, yh, hh = (sums[k : k + 1, :] for k in range(6))
    cx = 1.0 / jnp.sqrt(xx + EPS)
    cy = cx / SCALE
    vv, vi, ii = xx * cx * cx, xy * cx * cy, yy * cy * cy
    vh, ih, hh = xh * cx * cy, yh * cy * cy, hh * cy * cy
    alpha0 = vi
    square0 = ii - 2.0 * alpha0 * vi + alpha0 * alpha0 * vv
    beta0 = jnp.sqrt(jnp.maximum(square0, 0.0) + EPS)
    inv = 1.0 / beta0
    ui = (ii - alpha0 * vi) * inv
    uh = (ih - alpha0 * vh) * inv
    uv = (vi - alpha0 * vv) * inv
    uu = (ui - alpha0 * uv) * inv
    jv = (vh - alpha0 * vi) * inv
    jj = (hh - 2.0 * alpha0 * ih + alpha0 * alpha0 * ii) * inv * inv
    alpha1 = (uh - alpha0 * ui) * inv
    square1 = (
        jj + alpha1 * alpha1 * uu + beta0 * beta0 * vv
        - 2.0 * alpha1 * alpha1 - 2.0 * beta0 * jv + 2.0 * alpha1 * beta0 * uv
    )
    beta1 = jnp.sqrt(jnp.maximum(square1, 0.0) + EPS)
    last = 1.0 / beta1
    ch = inv * last * cy
    ci = -(alpha0 + alpha1) * inv * last * cy
    cv = (alpha1 * alpha0 * inv - beta0) * last * cx
    vector[0] = ch * h_ref[...] + ci * y_ref[...] + cv * x_ref[0].astype(jnp.float32)
    alphas[0], alphas[1] = alpha0[0, 0], alpha1[0, 0]
    betas[0], betas[1] = beta0[0, 0], beta1[0, 0]


def on_device(theta, left_env, right_env, term_shift, term_on, block_rows, block_cols):
    rows, width = theta.shape[1:]
    sec_count, term_count = lax.axis_size("sec"), lax.axis_size("term")
    sec, term = lax.axis_index("sec"), lax.axis_index("term")
    row = term * rows + lax.broadcasted_iota(jnp.int32, (1, rows, width), 1)
    col = lax.broadcasted_iota(jnp.int32, (1, rows, width), 2)
    start = jnp.where((row < block_rows[0]) & (col < block_cols[0]), theta, jnp.zeros_like(theta))
    toward_pair = 1 - 2 * (sec % 2)
    source = jnp.where(term_shift == 0, 0, jnp.where(term_shift == toward_pair, 1, 2))
    scal = jnp.concatenate(
        [source, term_on[:, 0], jnp.stack([term // 2, term % 2]), block_rows, block_cols]
    ).astype(jnp.int32)

    vmem, smem = (pl.BlockSpec(memory_space=m) for m in (pltpu.VMEM, pltpu.SMEM))
    small = pltpu.CompilerParams(vmem_limit_bytes=8 * 2**20)
    block = jax.ShapeDtypeStruct((rows, width), jnp.float32)
    tile = jax.ShapeDtypeStruct((8, 128), jnp.float32)
    pair = jax.ShapeDtypeStruct((2,), jnp.float32)

    pieces, scal = gather_pieces(start, scal, sec_count, term_count)
    mine, theirs = apply_terms(scal, left_env, right_env, pieces, rows)
    own, got = reduce_parts(mine, theirs, term_count)
    y, shard, sums = pl.pallas_call(
        image_kernel,
        out_shape=(block, jax.ShapeDtypeStruct((1, rows, width), jnp.bfloat16), tile),
        in_specs=[vmem] * (2 + len(got)),
        out_specs=(vmem,) * 3,
        compiler_params=small,
        name="image",
    )(start, own, *got)
    pieces, _ = gather_pieces(shard, (), sec_count, term_count)
    mine, theirs = apply_terms(scal, left_env, right_env, pieces, rows)
    own, got = reduce_parts(mine, theirs, term_count)
    h, sums = pl.pallas_call(
        gram_kernel,
        out_shape=(block, tile),
        in_specs=[vmem] * (4 + len(got)),
        out_specs=(vmem, vmem),
        compiler_params=small,
        name="gram",
    )(sums, start, y, own, *got)
    sums = everyones(sums, sec_count * term_count)
    vector, alphas, betas = pl.pallas_call(
        finish_kernel,
        out_shape=(jax.ShapeDtypeStruct((1, rows, width), jnp.float32), pair, pair),
        in_specs=[vmem] * 4,
        out_specs=(vmem, smem, smem),
        compiler_params=small,
        name="finish",
    )(sums, start, y, h)
    return (vector, alphas, betas)


def solution(mesh):
    return jax.shard_map(
        on_device,
        mesh=mesh,
        in_specs=(
            P("sec", "term", None),
            P("term", "sec", None, None),
            P("term", "sec", None, None),
            P("term"),
            P("term", "sec"),
            P("sec"),
            P("sec"),
        ),
        out_specs=(P("sec", "term", None), P(), P()),
        check_vma=False,
    )
```

```python
import functools

import jax
import jax.numpy as jnp
from jax import lax
from jax.experimental import pallas as pl
from jax.experimental.pallas import tpu as pltpu
from jax.sharding import PartitionSpec as P

ITERS = 2


EPS = 1e-06

SCALE = 2.0**-10


def along_term(x, partner, count):
    return lax.ppermute(x, "term", [(i, partner(i)) for i in range(count)])


def pair_exchange(x, count):
    return lax.ppermute(x, "sec", [(i, i ^ 1) for i in range(count) if (i ^ 1) < count])


def pair_forward(x, count):
    pairs = [(i, i + 2) for i in range(0, count, 2) if i + 2 < count]
    pairs += [(i, i - 2) for i in range(1, count, 2) if i >= 2]
    return lax.ppermute(x, "sec", pairs)


def across_pairs(x, count):
    pairs = [(i, i + 1) for i in range(1, count - 1, 2)]
    return lax.ppermute(x, "sec", pairs + [(j, i) for i, j in pairs])


def after(x, *others):
    return lax.optimization_barrier((x,) + others)[0]


FIRST = {
    "routes": {},
    "after": {"B1": ("p3",), "cA3": ("A1",), "p1": ("p2",)},
    "order": (),
}
SECOND = {
    "routes": {"B0": ("A0", "forward")},
    "after": {"B1": ("p3",), "cA3": ("A1",)},
    "order": (),
}


def default_routes(chips):
    last = chips - 1
    routes = {}
    for i in sorted(range(1, chips), key=lambda i: (bin(i).count("1"), i)):
        routes[f"p{i}"] = (f"p{i ^ (i & -i)}", i & -i)
    for i in range(chips):
        routes[f"A{i}"] = (f"p{i}", "pair") if i < last else (f"A{i ^ 1}", 1)
    for i in range(chips):
        near = (f"p{i}", "across") if i < chips // 2 else (f"A{i}", "forward")
        routes[f"B{i}"] = near if i < last else (f"B{i ^ 1}", 1)
    return routes


def gather_pieces(shard, beside, plan, sec_count, term_count):
    chips = term_count // 2
    routes, waits = default_routes(chips), {}
    if chips == 4 and sec_count == 4:
        routes.update(plan["routes"])
        waits = plan["after"]
    across = {"pair": pair_exchange, "forward": pair_forward, "across": across_pairs}
    got = {"p0": shard}

    def fetch(name):
        if name in got:
            return got[name]
        if name[0] == "c":
            origin, way = name[1:], 0
        else:
            origin, way = routes[name]
        x = fetch(origin)
        held = tuple(fetch(other) for other in waits.get(name, ()))
        if held:
            x = after(x, *held)
        if way in across:
            x = across[way](x, sec_count)
        else:
            x = along_term(x, lambda t: t ^ (2 * way or 1), term_count)
        if name == "p1":
            x, got["beside"] = lax.optimization_barrier((x, beside))
        got[name] = x
        return x

    for name in routes:
        fetch(name)
    names = [f"{source}{i}" for source in "pAB" for i in range(chips)]
    pieces = [piece for name in names for piece in (fetch(name), fetch("c" + name))]
    return pieces, got["beside"]


def operand_order(pieces, plan):
    order = plan["order"]
    return order if len(order) == len(pieces) else tuple(range(len(pieces)))


def apply_kernel(chips, terms, rows, order, scal, left, right, *refs):
    pieces = dict(zip(order, refs))
    mine, theirs, x_s, l_s, r_s, a_s, l_sem, r_sem = refs[6 * chips :]
    width = x_s.shape[2]
    z, c = scal[2 * terms], scal[2 * terms + 1]
    block_rows, block_cols = scal[2 * terms + 2], scal[2 * terms + 3]

    def l_copy(w):
        return pltpu.make_async_copy(left.at[w, 0], l_s.at[w], l_sem.at[w])

    def r_copy(w):
        return pltpu.make_async_copy(right.at[w, 0], r_s.at[pl.ds(w * width, width)], r_sem.at[w])

    for w in range(terms):
        l_copy(w).start()
    for w in range(terms):
        r_copy(w).start()
    for w in range(terms):
        for source in range(3):

            @pl.when(scal[w] == source)
            def _():
                for i in range(chips):
                    for other in range(2):
                        t = jnp.bitwise_xor(z, i) * 2 + jnp.bitwise_xor(c, other)
                        piece = pieces[source * 2 * chips + 2 * i + other]
                        x_s[w, pl.ds(pl.multiple_of(t * rows, rows), rows), :] = piece[0]

    for w in range(terms):
        on = scal[terms + w].astype(jnp.float32)
        l_copy(w).wait()
        product = jnp.dot(l_s[w], x_s[w], preferred_element_type=jnp.float32)
        a_s[:, w * width : (w + 1) * width] = (product * on).astype(jnp.bfloat16)
    for w in range(terms):
        r_copy(w).wait()
    col = lax.broadcasted_iota(jnp.int32, (2 * rows, width), 1)
    row = lax.broadcasted_iota(jnp.int32, (2 * rows, width), 0)
    for i in range(chips):
        start = pl.multiple_of(jnp.bitwise_xor(z, i) * 2 * rows, 2 * rows)
        total = jnp.dot(
            a_s[pl.ds(start, 2 * rows), :], r_s[...], preferred_element_type=jnp.float32
        )
        inside = (row + start < block_rows) & (col < block_cols)
        total = jnp.where(inside, total, 0.0)
        first = c == 0
        mine[i] = jnp.where(first, total[:rows], total[rows:])
        theirs[i] = jnp.where(first, total[rows:], total[:rows]).astype(theirs.dtype)


def apply_terms(scal, left_env, right_env, pieces, plan, rows):
    terms, _, width, _ = left_env.shape
    chips = len(pieces) // 6
    order = operand_order(pieces, plan)
    smem, hbm, vmem = (
        pl.BlockSpec(memory_space=m) for m in (pltpu.SMEM, pltpu.HBM, pltpu.VMEM)
    )
    return pl.pallas_call(
        functools.partial(apply_kernel, chips, terms, rows, order),
        out_shape=(
            jax.ShapeDtypeStruct((chips, rows, width), jnp.float32),
            jax.ShapeDtypeStruct((chips, rows, width), jnp.bfloat16),
        ),
        in_specs=[smem, hbm, hbm] + [vmem] * len(pieces),
        out_specs=(vmem, vmem),
        scratch_shapes=[
            pltpu.VMEM((terms, width, width), jnp.bfloat16),
            pltpu.VMEM((terms, width, width), jnp.bfloat16),
            pltpu.VMEM((terms * width, width), jnp.bfloat16),
            pltpu.VMEM((width, terms * width), jnp.bfloat16),
            pltpu.SemaphoreType.DMA((terms,)),
            pltpu.SemaphoreType.DMA((terms,)),
        ],
        compiler_params=pltpu.CompilerParams(vmem_limit_bytes=46 * 2**20),
        name="apply_terms",
    )(scal, left_env, right_env, *(pieces[k] for k in order))


def chip_kernel(chips, terms, rows, order, scal, theirs, *refs):
    lefts, rights, pieces = refs[:2], refs[2:4], dict(zip(order, refs[4:]))
    own, *parts = refs[4 + 6 * chips : 4 + 7 * chips]
    x_s, l_s, r_s, a_s, l_sem, r_sem = refs[4 + 7 * chips :]
    width = x_s.shape[2]
    z, c, block_rows, block_cols = (scal[2 * terms + k] for k in range(4))

    def offset(i, core):
        return pl.multiple_of((jnp.bitwise_xor(z, i) * 2 + core) * rows, rows)

    def l_copy(w, i):
        band = pl.ds(offset(i, c), rows)
        return pltpu.make_async_copy(
            lefts[w // terms].at[w % terms, 0, band],
            l_s.at[w, pl.ds(i * rows, rows)],
            l_sem.at[w],
        )

    def r_copy(w):
        return pltpu.make_async_copy(
            rights[w // terms].at[w % terms, 0], r_s.at[pl.ds(w * width, width)], r_sem.at[w]
        )

    for w in range(2 * terms):
        for i in range(chips):
            l_copy(w, i).start()
    for w in range(2 * terms):
        r_copy(w).start()
    for source in range(3):
        for i in range(chips):
            for other in range(2):
                band = pl.ds(offset(i, jnp.bitwise_xor(c, other)), rows)
                x_s[source, band, :] = pieces[source * 2 * chips + 2 * i + other][0]
    for w in range(2 * terms):
        table = theirs if w >= terms else scal
        source, on = table[w % terms], table[terms + w % terms].astype(jnp.float32)
        for i in range(chips):
            l_copy(w, i).wait()
        product = jnp.dot(l_s[w], x_s[source], preferred_element_type=jnp.float32)
        a_s[:, w * width : (w + 1) * width] = (product * on).astype(jnp.bfloat16)
    for w in range(2 * terms):
        r_copy(w).wait()
    total = jnp.dot(a_s[...], r_s[...], preferred_element_type=jnp.float32)
    col = lax.broadcasted_iota(jnp.int32, (rows, width), 1)
    row = lax.broadcasted_iota(jnp.int32, (rows, width), 0)
    for i in range(chips):
        inside = (row + offset(i, c) < block_rows) & (col < block_cols)
        band = jnp.where(inside, total[i * rows : (i + 1) * rows], 0.0)
        if i:
            parts[i - 1][...] = band.astype(jnp.bfloat16)
        else:
            own[...] = band


def apply_chip_terms(scal, theirs, envs, pieces, plan, rows):
    terms, _, width, _ = envs[0].shape
    chips = len(pieces) // 6
    order = operand_order(pieces, plan)
    smem, hbm, vmem = (
        pl.BlockSpec(memory_space=m) for m in (pltpu.SMEM, pltpu.HBM, pltpu.VMEM)
    )
    own, *parts = pl.pallas_call(
        functools.partial(chip_kernel, chips, terms, rows, order),
        out_shape=[jax.ShapeDtypeStruct((rows, width), jnp.float32)]
        + [jax.ShapeDtypeStruct((rows, width), jnp.bfloat16)] * (chips - 1),
        in_specs=[smem] * 2 + [hbm] * 4 + [vmem] * len(pieces),
        out_specs=[vmem] * chips,
        scratch_shapes=[
            pltpu.VMEM((3, width, width), jnp.bfloat16),
            pltpu.VMEM((2 * terms, chips * rows, width), jnp.bfloat16),
            pltpu.VMEM((2 * terms * width, width), jnp.bfloat16),
            pltpu.VMEM((chips * rows, 2 * terms * width), jnp.bfloat16),
            pltpu.SemaphoreType.DMA((2 * terms,)),
            pltpu.SemaphoreType.DMA((2 * terms,)),
        ],
        compiler_params=pltpu.CompilerParams(vmem_limit_bytes=46 * 2**20),
        name="apply_chip_terms",
    )(scal, theirs, *envs, *(pieces[k] for k in order))
    return own, parts


def reduce_parts(mine, theirs, term_count):
    other = along_term(theirs, lambda t: t ^ 1, term_count)
    totals = [mine[i] + other[i].astype(jnp.float32) for i in range(term_count // 2)]
    parts = [
        along_term(totals[i].astype(jnp.bfloat16), lambda t, b=i: t ^ (2 * b), term_count)
        for i in range(1, term_count // 2)
    ]
    return totals[0], parts


def send_parts(parts, term_count):
    sent = [
        along_term(parts[i - 1], lambda t, b=i: t ^ (2 * b), term_count)
        for i in range(len(parts), 0, -1)
    ]
    return sent[::-1]


def everyones(tile, count):
    return lax.all_to_all(jnp.broadcast_to(tile, (count,) + tile.shape), ("sec", "term"), 0, 0)


def lane_sums(tile, products):
    for k, (a, b) in products.items():
        line = jnp.sum(a * b, axis=0, keepdims=True)
        tile[k : k + 1, :] = sum(line[:, j : j + 128] for j in range(0, line.shape[1], 128))


def image_kernel(x_ref, own, *refs):
    y_ref, shard, tile = refs[-3:]
    y = own[...]
    for part in refs[:-3]:
        y = y + part[...].astype(jnp.float32)
    y = y * SCALE
    y_ref[...] = y
    shard[0] = y.astype(jnp.bfloat16)
    x = x_ref[0].astype(jnp.float32)
    tile[...] = jnp.zeros_like(tile)
    lane_sums(tile, {0: (x, x), 1: (x, y), 2: (y, y)})


def gram_kernel(before, x_ref, y_ref, own, *refs):
    h_ref, tile = refs[-2:]
    h = own[...]
    for part in refs[:-2]:
        h = h + part[...].astype(jnp.float32)
    h_ref[...] = h
    x, y = x_ref[0].astype(jnp.float32), y_ref[...]
    tile[...] = before[...]
    lane_sums(tile, {3: (x, h), 4: (y, h), 5: (h, h)})


def finish_kernel(tiles, x_ref, y_ref, h_ref, vector, alphas, betas):
    sums = jnp.sum(jnp.sum(tiles[...], axis=0), axis=1, keepdims=True)
    xx, xy, yy, xh, yh, hh = (sums[k : k + 1, :] for k in range(6))
    cx = 1.0 / jnp.sqrt(xx + EPS)
    cy = cx / SCALE
    vv, vi, ii = xx * cx * cx, xy * cx * cy, yy * cy * cy
    vh, ih, hh = xh * cx * cy, yh * cy * cy, hh * cy * cy
    alpha0 = vi
    square0 = ii - 2.0 * alpha0 * vi + alpha0 * alpha0 * vv
    beta0 = jnp.sqrt(jnp.maximum(square0, 0.0) + EPS)
    inv = 1.0 / beta0
    ui = (ii - alpha0 * vi) * inv
    uh = (ih - alpha0 * vh) * inv
    uv = (vi - alpha0 * vv) * inv
    uu = (ui - alpha0 * uv) * inv
    jv = (vh - alpha0 * vi) * inv
    jj = (hh - 2.0 * alpha0 * ih + alpha0 * alpha0 * ii) * inv * inv
    alpha1 = (uh - alpha0 * ui) * inv
    square1 = (
        jj + alpha1 * alpha1 * uu + beta0 * beta0 * vv
        - 2.0 * alpha1 * alpha1 - 2.0 * beta0 * jv + 2.0 * alpha1 * beta0 * uv
    )
    beta1 = jnp.sqrt(jnp.maximum(square1, 0.0) + EPS)
    last = 1.0 / beta1
    ch = inv * last * cy
    ci = -(alpha0 + alpha1) * inv * last * cy
    cv = (alpha1 * alpha0 * inv - beta0) * last * cx
    vector[0] = ch * h_ref[...] + ci * y_ref[...] + cv * x_ref[0].astype(jnp.float32)
    alphas[0], alphas[1] = alpha0[0, 0], alpha1[0, 0]
    betas[0], betas[1] = beta0[0, 0], beta1[0, 0]


def on_device(theta, left_env, right_env, term_shift, term_on, block_rows, block_cols):
    rows, width = theta.shape[1:]
    terms = left_env.shape[0]
    sec_count, term_count = lax.axis_size("sec"), lax.axis_size("term")
    sec, term = lax.axis_index("sec"), lax.axis_index("term")
    row = term * rows + lax.broadcasted_iota(jnp.int32, (1, rows, width), 1)
    col = lax.broadcasted_iota(jnp.int32, (1, rows, width), 2)
    start = jnp.where((row < block_rows[0]) & (col < block_cols[0]), theta, jnp.zeros_like(theta))
    toward_pair = 1 - 2 * (sec % 2)
    source = jnp.where(term_shift == 0, 0, jnp.where(term_shift == toward_pair, 1, 2))
    scal = jnp.concatenate(
        [source, term_on[:, 0], jnp.stack([term // 2, term % 2]), block_rows, block_cols]
    ).astype(jnp.int32)

    vmem, smem = (pl.BlockSpec(memory_space=m) for m in (pltpu.VMEM, pltpu.SMEM))
    small = pltpu.CompilerParams(vmem_limit_bytes=8 * 2**20)
    block = jax.ShapeDtypeStruct((rows, width), jnp.float32)
    tile = jax.ShapeDtypeStruct((8, 128), jnp.float32)
    pair = jax.ShapeDtypeStruct((2,), jnp.float32)

    pieces, scal = gather_pieces(start, scal, FIRST, sec_count, term_count)
    mine, theirs = apply_terms(scal, left_env, right_env, pieces, FIRST, rows)
    own, got = reduce_parts(mine, theirs, term_count)
    local = lax.optimization_barrier((left_env, right_env, scal[: 2 * terms], own))[:3]
    swapped = [along_term(a, lambda t: t ^ 1, term_count) for a in local]
    own, swapped = lax.optimization_barrier((own, swapped))
    envs = (left_env, swapped[0], right_env, swapped[1])
    y, shard, sums = pl.pallas_call(
        image_kernel,
        out_shape=(block, jax.ShapeDtypeStruct((1, rows, width), jnp.bfloat16), tile),
        in_specs=[vmem] * (2 + len(got)),
        out_specs=(vmem,) * 3,
        compiler_params=small,
        name="image",
    )(start, own, *got)
    pieces, _ = gather_pieces(shard, (), SECOND, sec_count, term_count)
    own, parts = apply_chip_terms(scal, swapped[2], envs, pieces, SECOND, rows)
    got = send_parts(parts, term_count)
    h, sums = pl.pallas_call(
        gram_kernel,
        out_shape=(block, tile),
        in_specs=[vmem] * (4 + len(got)),
        out_specs=(vmem, vmem),
        compiler_params=small,
        name="gram",
    )(sums, start, y, own, *got[::-1])
    sums = everyones(sums, sec_count * term_count)
    vector, alphas, betas = pl.pallas_call(
        finish_kernel,
        out_shape=(jax.ShapeDtypeStruct((1, rows, width), jnp.float32), pair, pair),
        in_specs=[vmem] * 4,
        out_specs=(vmem, smem, smem),
        compiler_params=small,
        name="finish",
    )(sums, start, y, h)
    return (vector, alphas, betas)


def solution(mesh):
    return jax.shard_map(
        on_device,
        mesh=mesh,
        in_specs=(
            P("sec", "term", None),
            P("term", "sec", None, None),
            P("term", "sec", None, None),
            P("term"),
            P("term", "sec"),
            P("sec"),
            P("sec"),
        ),
        out_specs=(P("sec", "term", None), P(), P()),
        check_vma=False,
    )
```

```python
import functools

import jax
import jax.numpy as jnp
from jax import lax
from jax.experimental import pallas as pl
from jax.experimental.pallas import tpu as pltpu
from jax.sharding import PartitionSpec as P

ITERS = 2


EPS = 1e-06

SCALE = 2.0**-10


def along_term(x, partner, count):
    return lax.ppermute(x, "term", [(i, partner(i)) for i in range(count)])


def pair_exchange(x, count):
    return lax.ppermute(x, "sec", [(i, i ^ 1) for i in range(count) if (i ^ 1) < count])


def pair_forward(x, count):
    pairs = [(i, i + 2) for i in range(0, count, 2) if i + 2 < count]
    pairs += [(i, i - 2) for i in range(1, count, 2) if i >= 2]
    return lax.ppermute(x, "sec", pairs)


def across_pairs(x, count):
    pairs = [(i, i + 1) for i in range(1, count - 1, 2)]
    return lax.ppermute(x, "sec", pairs + [(j, i) for i, j in pairs])


def after(x, *others):
    return lax.optimization_barrier((x,) + others)[0]


FIRST = {
    "routes": {},
    "after": {"B1": ("p3",)},
    "order": (),
}
SECOND = {
    "routes": {"B0": ("A0", "forward")},
    "after": {"B1": ("A2",), "cA3": ("A1",)},
    "order": (),
}


def default_routes(chips):
    last = chips - 1
    routes = {}
    for i in sorted(range(1, chips), key=lambda i: (bin(i).count("1"), i)):
        routes[f"p{i}"] = (f"p{i ^ (i & -i)}", i & -i)
    for i in range(chips):
        routes[f"A{i}"] = (f"p{i}", "pair") if i < last else (f"A{i ^ 1}", 1)
    for i in range(chips):
        near = (f"p{i}", "across") if i < chips // 2 else (f"A{i}", "forward")
        routes[f"B{i}"] = near if i < last else (f"B{i ^ 1}", 1)
    return routes


def gather_pieces(shard, beside, plan, sec_count, term_count):
    chips = term_count // 2
    routes, waits = default_routes(chips), {}
    if chips == 4 and sec_count == 4:
        routes.update(plan["routes"])
        waits = plan["after"]
    across = {"pair": pair_exchange, "forward": pair_forward, "across": across_pairs}
    got = {"p0": shard}

    def fetch(name):
        if name in got:
            return got[name]
        if name[0] == "c":
            origin, way = name[1:], 0
        else:
            origin, way = routes[name]
        x = fetch(origin)
        held = tuple(fetch(other) for other in waits.get(name, ()))
        if held:
            x = after(x, *held)
        if way in across:
            x = across[way](x, sec_count)
        else:
            x = along_term(x, lambda t: t ^ (2 * way or 1), term_count)
        if name == "p1":
            x, got["beside"] = lax.optimization_barrier((x, beside))
        got[name] = x
        return x

    for name in routes:
        fetch(name)
    names = [f"{source}{i}" for source in "pAB" for i in range(chips)]
    pieces = [piece for name in names for piece in (fetch(name), fetch("c" + name))]
    return pieces, got["beside"]


def operand_order(pieces, plan):
    order = plan["order"]
    return order if len(order) == len(pieces) else tuple(range(len(pieces)))


def apply_kernel(chips, terms, rows, order, scal, left, right, *refs):
    pieces = dict(zip(order, refs))
    mine, theirs, x_s, l_s, r_s, a_s, l_sem, r_sem = refs[6 * chips :]
    width = x_s.shape[2]
    z, c = scal[2 * terms], scal[2 * terms + 1]
    block_rows, block_cols = scal[2 * terms + 2], scal[2 * terms + 3]

    def l_copy(w):
        return pltpu.make_async_copy(left.at[w, 0], l_s.at[w], l_sem.at[w])

    def r_copy(w):
        return pltpu.make_async_copy(right.at[w, 0], r_s.at[pl.ds(w * width, width)], r_sem.at[w])

    for w in range(terms):
        l_copy(w).start()
    for w in range(terms):
        r_copy(w).start()
    for w in range(terms):
        for source in range(3):

            @pl.when(scal[w] == source)
            def _():
                for i in range(chips):
                    for other in range(2):
                        t = jnp.bitwise_xor(z, i) * 2 + jnp.bitwise_xor(c, other)
                        piece = pieces[source * 2 * chips + 2 * i + other]
                        x_s[w, pl.ds(pl.multiple_of(t * rows, rows), rows), :] = piece[0]

    for w in range(terms):
        on = scal[terms + w].astype(jnp.float32)
        l_copy(w).wait()
        product = jnp.dot(l_s[w], x_s[w], preferred_element_type=jnp.float32)
        a_s[:, w * width : (w + 1) * width] = (product * on).astype(jnp.bfloat16)
    for w in range(terms):
        r_copy(w).wait()
    col = lax.broadcasted_iota(jnp.int32, (2 * rows, width), 1)
    row = lax.broadcasted_iota(jnp.int32, (2 * rows, width), 0)
    for i in range(chips):
        start = pl.multiple_of(jnp.bitwise_xor(z, i) * 2 * rows, 2 * rows)
        total = jnp.dot(
            a_s[pl.ds(start, 2 * rows), :], r_s[...], preferred_element_type=jnp.float32
        )
        inside = (row + start < block_rows) & (col < block_cols)
        total = jnp.where(inside, total, 0.0)
        first = c == 0
        mine[i] = jnp.where(first, total[:rows], total[rows:])
        theirs[i] = jnp.where(first, total[rows:], total[:rows]).astype(theirs.dtype)


def apply_terms(scal, left_env, right_env, pieces, plan, rows):
    terms, _, width, _ = left_env.shape
    chips = len(pieces) // 6
    order = operand_order(pieces, plan)
    smem, hbm, vmem = (
        pl.BlockSpec(memory_space=m) for m in (pltpu.SMEM, pltpu.HBM, pltpu.VMEM)
    )
    return pl.pallas_call(
        functools.partial(apply_kernel, chips, terms, rows, order),
        out_shape=(
            jax.ShapeDtypeStruct((chips, rows, width), jnp.float32),
            jax.ShapeDtypeStruct((chips, rows, width), jnp.bfloat16),
        ),
        in_specs=[smem, hbm, hbm] + [vmem] * len(pieces),
        out_specs=(vmem, vmem),
        scratch_shapes=[
            pltpu.VMEM((terms, width, width), jnp.bfloat16),
            pltpu.VMEM((terms, width, width), jnp.bfloat16),
            pltpu.VMEM((terms * width, width), jnp.bfloat16),
            pltpu.VMEM((width, terms * width), jnp.bfloat16),
            pltpu.SemaphoreType.DMA((terms,)),
            pltpu.SemaphoreType.DMA((terms,)),
        ],
        compiler_params=pltpu.CompilerParams(vmem_limit_bytes=46 * 2**20),
        name="apply_terms",
    )(scal, left_env, right_env, *(pieces[k] for k in order))


def chip_kernel(chips, terms, rows, order, scal, theirs, *refs):
    lefts, rights, pieces = refs[:2], refs[2:4], dict(zip(order, refs[4:]))
    own, *parts = refs[4 + 6 * chips : 4 + 7 * chips]
    x_s, l_s, r_s, a_s, l_sem, r_sem = refs[4 + 7 * chips :]
    width = x_s.shape[2]
    z, c, block_rows, block_cols = (scal[2 * terms + k] for k in range(4))

    def offset(i, core):
        return pl.multiple_of((jnp.bitwise_xor(z, i) * 2 + core) * rows, rows)

    def l_copy(w, i):
        band = pl.ds(offset(i, c), rows)
        return pltpu.make_async_copy(
            lefts[w // terms].at[w % terms, 0, band],
            l_s.at[w, pl.ds(i * rows, rows)],
            l_sem.at[w],
        )

    def r_copy(w):
        return pltpu.make_async_copy(
            rights[w // terms].at[w % terms, 0], r_s.at[pl.ds(w * width, width)], r_sem.at[w]
        )

    for w in range(2 * terms):
        for i in range(chips):
            l_copy(w, i).start()
    for w in range(2 * terms):
        r_copy(w).start()
    for source in range(3):
        for i in range(chips):
            for other in range(2):
                band = pl.ds(offset(i, jnp.bitwise_xor(c, other)), rows)
                x_s[source, band, :] = pieces[source * 2 * chips + 2 * i + other][0]
    for w in range(2 * terms):
        table = theirs if w >= terms else scal
        source, on = table[w % terms], table[terms + w % terms].astype(jnp.float32)
        for i in range(chips):
            l_copy(w, i).wait()
        product = jnp.dot(l_s[w], x_s[source], preferred_element_type=jnp.float32)
        a_s[:, w * width : (w + 1) * width] = (product * on).astype(jnp.bfloat16)
    for w in range(2 * terms):
        r_copy(w).wait()
    total = jnp.dot(a_s[...], r_s[...], preferred_element_type=jnp.float32)
    col = lax.broadcasted_iota(jnp.int32, (rows, width), 1)
    row = lax.broadcasted_iota(jnp.int32, (rows, width), 0)
    for i in range(chips):
        inside = (row + offset(i, c) < block_rows) & (col < block_cols)
        band = jnp.where(inside, total[i * rows : (i + 1) * rows], 0.0)
        if i:
            parts[i - 1][...] = band.astype(jnp.bfloat16)
        else:
            own[...] = band


def apply_chip_terms(scal, theirs, envs, pieces, plan, rows):
    terms, _, width, _ = envs[0].shape
    chips = len(pieces) // 6
    order = operand_order(pieces, plan)
    smem, hbm, vmem = (
        pl.BlockSpec(memory_space=m) for m in (pltpu.SMEM, pltpu.HBM, pltpu.VMEM)
    )
    own, *parts = pl.pallas_call(
        functools.partial(chip_kernel, chips, terms, rows, order),
        out_shape=[jax.ShapeDtypeStruct((rows, width), jnp.float32)]
        + [jax.ShapeDtypeStruct((rows, width), jnp.bfloat16)] * (chips - 1),
        in_specs=[smem] * 2 + [hbm] * 4 + [vmem] * len(pieces),
        out_specs=[vmem] * chips,
        scratch_shapes=[
            pltpu.VMEM((3, width, width), jnp.bfloat16),
            pltpu.VMEM((2 * terms, chips * rows, width), jnp.bfloat16),
            pltpu.VMEM((2 * terms * width, width), jnp.bfloat16),
            pltpu.VMEM((chips * rows, 2 * terms * width), jnp.bfloat16),
            pltpu.SemaphoreType.DMA((2 * terms,)),
            pltpu.SemaphoreType.DMA((2 * terms,)),
        ],
        compiler_params=pltpu.CompilerParams(vmem_limit_bytes=46 * 2**20),
        name="apply_chip_terms",
    )(scal, theirs, *envs, *(pieces[k] for k in order))
    return own, parts


def reduce_parts(mine, theirs, term_count):
    other = along_term(theirs, lambda t: t ^ 1, term_count)
    totals = [mine[i] + other[i].astype(jnp.float32) for i in range(term_count // 2)]
    parts = [
        along_term(totals[i].astype(jnp.bfloat16), lambda t, b=i: t ^ (2 * b), term_count)
        for i in range(1, term_count // 2)
    ]
    return totals[0], parts


def send_parts(parts, term_count):
    sent = [
        along_term(parts[i - 1], lambda t, b=i: t ^ (2 * b), term_count)
        for i in range(len(parts), 0, -1)
    ]
    return sent[::-1]


def everyones(tile, count):
    return lax.all_to_all(jnp.broadcast_to(tile, (count,) + tile.shape), ("sec", "term"), 0, 0)


def lane_sums(tile, products):
    for k, (a, b) in products.items():
        line = jnp.sum(a * b, axis=0, keepdims=True)
        tile[k : k + 1, :] = sum(line[:, j : j + 128] for j in range(0, line.shape[1], 128))


def image_kernel(x_ref, own, *refs):
    y_ref, shard, tile = refs[-3:]
    y = own[...]
    for part in refs[:-3]:
        y = y + part[...].astype(jnp.float32)
    y = y * SCALE
    y_ref[...] = y
    shard[0] = y.astype(jnp.bfloat16)
    x = x_ref[0].astype(jnp.float32)
    tile[...] = jnp.zeros_like(tile)
    lane_sums(tile, {0: (x, x), 1: (x, y), 2: (y, y)})


def gram_kernel(before, x_ref, y_ref, own, *refs):
    h_ref, tile = refs[-2:]
    h = own[...]
    for part in refs[:-2]:
        h = h + part[...].astype(jnp.float32)
    h_ref[...] = h
    x, y = x_ref[0].astype(jnp.float32), y_ref[...]
    tile[...] = before[...]
    lane_sums(tile, {3: (x, h), 4: (y, h), 5: (h, h)})


def finish_kernel(tiles, x_ref, y_ref, h_ref, vector, alphas, betas):
    sums = jnp.sum(jnp.sum(tiles[...], axis=0), axis=1, keepdims=True)
    xx, xy, yy, xh, yh, hh = (sums[k : k + 1, :] for k in range(6))
    cx = 1.0 / jnp.sqrt(xx + EPS)
    cy = cx / SCALE
    vv, vi, ii = xx * cx * cx, xy * cx * cy, yy * cy * cy
    vh, ih, hh = xh * cx * cy, yh * cy * cy, hh * cy * cy
    alpha0 = vi
    square0 = ii - 2.0 * alpha0 * vi + alpha0 * alpha0 * vv
    beta0 = jnp.sqrt(jnp.maximum(square0, 0.0) + EPS)
    inv = 1.0 / beta0
    ui = (ii - alpha0 * vi) * inv
    uh = (ih - alpha0 * vh) * inv
    uv = (vi - alpha0 * vv) * inv
    uu = (ui - alpha0 * uv) * inv
    jv = (vh - alpha0 * vi) * inv
    jj = (hh - 2.0 * alpha0 * ih + alpha0 * alpha0 * ii) * inv * inv
    alpha1 = (uh - alpha0 * ui) * inv
    square1 = (
        jj + alpha1 * alpha1 * uu + beta0 * beta0 * vv
        - 2.0 * alpha1 * alpha1 - 2.0 * beta0 * jv + 2.0 * alpha1 * beta0 * uv
    )
    beta1 = jnp.sqrt(jnp.maximum(square1, 0.0) + EPS)
    last = 1.0 / beta1
    ch = inv * last * cy
    ci = -(alpha0 + alpha1) * inv * last * cy
    cv = (alpha1 * alpha0 * inv - beta0) * last * cx
    vector[0] = ch * h_ref[...] + ci * y_ref[...] + cv * x_ref[0].astype(jnp.float32)
    alphas[0], alphas[1] = alpha0[0, 0], alpha1[0, 0]
    betas[0], betas[1] = beta0[0, 0], beta1[0, 0]


def on_device(theta, left_env, right_env, term_shift, term_on, block_rows, block_cols):
    rows, width = theta.shape[1:]
    terms = left_env.shape[0]
    sec_count, term_count = lax.axis_size("sec"), lax.axis_size("term")
    sec, term = lax.axis_index("sec"), lax.axis_index("term")
    row = term * rows + lax.broadcasted_iota(jnp.int32, (1, rows, width), 1)
    col = lax.broadcasted_iota(jnp.int32, (1, rows, width), 2)
    start = jnp.where((row < block_rows[0]) & (col < block_cols[0]), theta, jnp.zeros_like(theta))
    toward_pair = 1 - 2 * (sec % 2)
    source = jnp.where(term_shift == 0, 0, jnp.where(term_shift == toward_pair, 1, 2))
    scal = jnp.concatenate(
        [source, term_on[:, 0], jnp.stack([term // 2, term % 2]), block_rows, block_cols]
    ).astype(jnp.int32)

    vmem, smem = (pl.BlockSpec(memory_space=m) for m in (pltpu.VMEM, pltpu.SMEM))
    small = pltpu.CompilerParams(vmem_limit_bytes=8 * 2**20)
    block = jax.ShapeDtypeStruct((rows, width), jnp.float32)
    tile = jax.ShapeDtypeStruct((8, 128), jnp.float32)
    pair = jax.ShapeDtypeStruct((2,), jnp.float32)

    pieces, scal = gather_pieces(start, scal, FIRST, sec_count, term_count)
    mine, theirs = apply_terms(scal, left_env, right_env, pieces, FIRST, rows)
    own, got = reduce_parts(mine, theirs, term_count)
    local = lax.optimization_barrier((left_env, right_env, scal[: 2 * terms], own))[:3]
    swapped = [along_term(a, lambda t: t ^ 1, term_count) for a in local]
    own, swapped = lax.optimization_barrier((own, swapped))
    envs = (left_env, swapped[0], right_env, swapped[1])
    y, shard, sums = pl.pallas_call(
        image_kernel,
        out_shape=(block, jax.ShapeDtypeStruct((1, rows, width), jnp.bfloat16), tile),
        in_specs=[vmem] * (2 + len(got)),
        out_specs=(vmem,) * 3,
        compiler_params=small,
        name="image",
    )(start, own, *got)
    pieces, _ = gather_pieces(shard, (), SECOND, sec_count, term_count)
    own, parts = apply_chip_terms(scal, swapped[2], envs, pieces, SECOND, rows)
    got = send_parts(parts, term_count)
    h, sums = pl.pallas_call(
        gram_kernel,
        out_shape=(block, tile),
        in_specs=[vmem] * (4 + len(got)),
        out_specs=(vmem, vmem),
        compiler_params=small,
        name="gram",
    )(sums, start, y, own, *got[::-1])
    sums = everyones(sums, sec_count * term_count)
    vector, alphas, betas = pl.pallas_call(
        finish_kernel,
        out_shape=(jax.ShapeDtypeStruct((1, rows, width), jnp.float32), pair, pair),
        in_specs=[vmem] * 4,
        out_specs=(vmem, smem, smem),
        compiler_params=small,
        name="finish",
    )(sums, start, y, h)
    return (vector, alphas, betas)


def solution(mesh):
    return jax.shard_map(
        on_device,
        mesh=mesh,
        in_specs=(
            P("sec", "term", None),
            P("term", "sec", None, None),
            P("term", "sec", None, None),
            P("term"),
            P("term", "sec"),
            P("sec"),
            P("sec"),
        ),
        out_specs=(P("sec", "term", None), P(), P()),
        check_vma=False,
    )
```

```python
import functools

import jax
import jax.numpy as jnp
from jax import lax
from jax.experimental import pallas as pl
from jax.experimental.pallas import tpu as pltpu
from jax.sharding import PartitionSpec as P

ITERS = 2


EPS = 1e-06

SCALE = 2.0**-10


def along_term(x, partner, count):
    return lax.ppermute(x, "term", [(i, partner(i)) for i in range(count)])


def pair_exchange(x, count):
    return lax.ppermute(x, "sec", [(i, i ^ 1) for i in range(count) if (i ^ 1) < count])


def pair_forward(x, count):
    pairs = [(i, i + 2) for i in range(0, count, 2) if i + 2 < count]
    pairs += [(i, i - 2) for i in range(1, count, 2) if i >= 2]
    return lax.ppermute(x, "sec", pairs)


def across_pairs(x, count):
    pairs = [(i, i + 1) for i in range(1, count - 1, 2)]
    return lax.ppermute(x, "sec", pairs + [(j, i) for i, j in pairs])


def after(x, *others):
    return lax.optimization_barrier((x,) + others)[0]


FIRST = {
    "routes": {},
    "after": {"B1": ("p3",)},
    "order": (),
}
SECOND = {
    "routes": {"B0": ("A0", "forward")},
    "after": {"B1": ("A2",), "cA3": ("A1",)},
    "order": (),
}


def default_routes(chips):
    last = chips - 1
    routes = {}
    for i in sorted(range(1, chips), key=lambda i: (bin(i).count("1"), i)):
        routes[f"p{i}"] = (f"p{i ^ (i & -i)}", i & -i)
    for i in range(chips):
        routes[f"A{i}"] = (f"p{i}", "pair") if i < last else (f"A{i ^ 1}", 1)
    for i in range(chips):
        near = (f"p{i}", "across") if i < chips // 2 else (f"A{i}", "forward")
        routes[f"B{i}"] = near if i < last else (f"B{i ^ 1}", 1)
    return routes


def gather_pieces(shard, beside, plan, sec_count, term_count):
    chips = term_count // 2
    routes, waits = default_routes(chips), {}
    if chips == 4 and sec_count == 4:
        routes.update(plan["routes"])
        waits = plan["after"]
    across = {"pair": pair_exchange, "forward": pair_forward, "across": across_pairs}
    got = {"p0": shard}

    def fetch(name):
        if name in got:
            return got[name]
        if name[0] == "c":
            origin, way = name[1:], 0
        else:
            origin, way = routes[name]
        x = fetch(origin)
        held = tuple(fetch(other) for other in waits.get(name, ()))
        if held:
            x = after(x, *held)
        if way in across:
            x = across[way](x, sec_count)
        else:
            x = along_term(x, lambda t: t ^ (2 * way or 1), term_count)
        if name == "p1":
            x, got["beside"] = lax.optimization_barrier((x, beside))
        got[name] = x
        return x

    for name in routes:
        fetch(name)
    names = [f"{source}{i}" for source in "pAB" for i in range(chips)]
    pieces = [piece for name in names for piece in (fetch(name), fetch("c" + name))]
    return pieces, got["beside"]


def operand_order(pieces, plan):
    order = plan["order"]
    return order if len(order) == len(pieces) else tuple(range(len(pieces)))


def apply_kernel(chips, terms, rows, order, scal, left, right, *refs):
    pieces = dict(zip(order, refs))
    mine, theirs, x_s, l_s, r_s, a_s, l_sem, r_sem = refs[6 * chips :]
    width = x_s.shape[2]
    z, c = scal[2 * terms], scal[2 * terms + 1]
    block_rows, block_cols = scal[2 * terms + 2], scal[2 * terms + 3]

    def l_copy(w):
        return pltpu.make_async_copy(left.at[w, 0], l_s.at[w], l_sem.at[w])

    def r_copy(w):
        return pltpu.make_async_copy(right.at[w, 0], r_s.at[pl.ds(w * width, width)], r_sem.at[w])

    for w in range(terms):
        l_copy(w).start()
    for w in range(terms):
        r_copy(w).start()
    for w in range(terms):
        for source in range(3):

            @pl.when(scal[w] == source)
            def _():
                for i in range(chips):
                    for other in range(2):
                        t = jnp.bitwise_xor(z, i) * 2 + jnp.bitwise_xor(c, other)
                        piece = pieces[source * 2 * chips + 2 * i + other]
                        x_s[w, pl.ds(pl.multiple_of(t * rows, rows), rows), :] = piece[0]

    for w in range(terms):
        on = scal[terms + w].astype(jnp.float32)
        l_copy(w).wait()
        product = jnp.dot(l_s[w], x_s[w], preferred_element_type=jnp.float32)
        a_s[:, w * width : (w + 1) * width] = (product * on).astype(jnp.bfloat16)
    for w in range(terms):
        r_copy(w).wait()
    col = lax.broadcasted_iota(jnp.int32, (2 * rows, width), 1)
    row = lax.broadcasted_iota(jnp.int32, (2 * rows, width), 0)
    for i in range(chips):
        start = pl.multiple_of(jnp.bitwise_xor(z, i) * 2 * rows, 2 * rows)
        total = jnp.dot(
            a_s[pl.ds(start, 2 * rows), :], r_s[...], preferred_element_type=jnp.float32
        )
        inside = (row + start < block_rows) & (col < block_cols)
        total = jnp.where(inside, total, 0.0)
        first = c == 0
        mine[i] = jnp.where(first, total[:rows], total[rows:])
        theirs[i] = jnp.where(first, total[rows:], total[:rows]).astype(theirs.dtype)


def apply_terms(scal, left_env, right_env, pieces, plan, rows):
    terms, _, width, _ = left_env.shape
    chips = len(pieces) // 6
    order = operand_order(pieces, plan)
    smem, hbm, vmem = (
        pl.BlockSpec(memory_space=m) for m in (pltpu.SMEM, pltpu.HBM, pltpu.VMEM)
    )
    return pl.pallas_call(
        functools.partial(apply_kernel, chips, terms, rows, order),
        out_shape=(
            jax.ShapeDtypeStruct((chips, rows, width), jnp.float32),
            jax.ShapeDtypeStruct((chips, rows, width), jnp.bfloat16),
        ),
        in_specs=[smem, hbm, hbm] + [vmem] * len(pieces),
        out_specs=(vmem, vmem),
        scratch_shapes=[
            pltpu.VMEM((terms, width, width), jnp.bfloat16),
            pltpu.VMEM((terms, width, width), jnp.bfloat16),
            pltpu.VMEM((terms * width, width), jnp.bfloat16),
            pltpu.VMEM((width, terms * width), jnp.bfloat16),
            pltpu.SemaphoreType.DMA((terms,)),
            pltpu.SemaphoreType.DMA((terms,)),
        ],
        compiler_params=pltpu.CompilerParams(vmem_limit_bytes=46 * 2**20),
        name="apply_terms",
    )(scal, left_env, right_env, *(pieces[k] for k in order))


def chip_kernel(chips, terms, rows, order, scal, theirs, *refs):
    lefts, rights, pieces = refs[:2], refs[2:4], dict(zip(order, refs[4:]))
    own, *parts = refs[4 + 6 * chips : 4 + 7 * chips]
    x_s, l_s, r_s, a_s, l_sem, r_sem = refs[4 + 7 * chips :]
    width = x_s.shape[2]
    z, c, block_rows, block_cols = (scal[2 * terms + k] for k in range(4))

    def offset(i, core):
        return pl.multiple_of((jnp.bitwise_xor(z, i) * 2 + core) * rows, rows)

    def l_copy(w, i):
        band = pl.ds(offset(i, c), rows)
        return pltpu.make_async_copy(
            lefts[w // terms].at[w % terms, 0, band],
            l_s.at[w, pl.ds(i * rows, rows)],
            l_sem.at[w],
        )

    def r_copy(w):
        return pltpu.make_async_copy(
            rights[w // terms].at[w % terms, 0], r_s.at[pl.ds(w * width, width)], r_sem.at[w]
        )

    for w in range(2 * terms):
        for i in range(chips):
            l_copy(w, i).start()
    for w in range(2 * terms):
        r_copy(w).start()
    for source in range(3):
        for i in range(chips):
            for other in range(2):
                band = pl.ds(offset(i, jnp.bitwise_xor(c, other)), rows)
                x_s[source, band, :] = pieces[source * 2 * chips + 2 * i + other][0]
    for w in range(2 * terms):
        table = theirs if w >= terms else scal
        source, on = table[w % terms], table[terms + w % terms].astype(jnp.float32)
        for i in range(chips):
            l_copy(w, i).wait()
        product = jnp.dot(l_s[w], x_s[source], preferred_element_type=jnp.float32)
        a_s[:, w * width : (w + 1) * width] = (product * on).astype(jnp.bfloat16)
    for w in range(2 * terms):
        r_copy(w).wait()
    total = jnp.dot(a_s[...], r_s[...], preferred_element_type=jnp.float32)
    col = lax.broadcasted_iota(jnp.int32, (rows, width), 1)
    row = lax.broadcasted_iota(jnp.int32, (rows, width), 0)
    for i in range(chips):
        inside = (row + offset(i, c) < block_rows) & (col < block_cols)
        band = jnp.where(inside, total[i * rows : (i + 1) * rows], 0.0)
        if i:
            parts[i - 1][...] = band.astype(jnp.bfloat16)
        else:
            own[...] = band


def apply_chip_terms(scal, theirs, envs, pieces, plan, rows):
    terms, _, width, _ = envs[0].shape
    chips = len(pieces) // 6
    order = operand_order(pieces, plan)
    smem, hbm, vmem = (
        pl.BlockSpec(memory_space=m) for m in (pltpu.SMEM, pltpu.HBM, pltpu.VMEM)
    )
    own, *parts = pl.pallas_call(
        functools.partial(chip_kernel, chips, terms, rows, order),
        out_shape=[jax.ShapeDtypeStruct((rows, width), jnp.float32)]
        + [jax.ShapeDtypeStruct((rows, width), jnp.bfloat16)] * (chips - 1),
        in_specs=[smem] * 2 + [hbm] * 4 + [vmem] * len(pieces),
        out_specs=[vmem] * chips,
        scratch_shapes=[
            pltpu.VMEM((3, width, width), jnp.bfloat16),
            pltpu.VMEM((2 * terms, chips * rows, width), jnp.bfloat16),
            pltpu.VMEM((2 * terms * width, width), jnp.bfloat16),
            pltpu.VMEM((chips * rows, 2 * terms * width), jnp.bfloat16),
            pltpu.SemaphoreType.DMA((2 * terms,)),
            pltpu.SemaphoreType.DMA((2 * terms,)),
        ],
        compiler_params=pltpu.CompilerParams(vmem_limit_bytes=46 * 2**20),
        name="apply_chip_terms",
    )(scal, theirs, *envs, *(pieces[k] for k in order))
    return own, parts


def reduce_parts(mine, theirs, term_count):
    other = along_term(theirs, lambda t: t ^ 1, term_count)
    totals = [mine[i] + other[i].astype(jnp.float32) for i in range(term_count // 2)]
    parts = [
        along_term(totals[i].astype(jnp.bfloat16), lambda t, b=i: t ^ (2 * b), term_count)
        for i in range(1, term_count // 2)
    ]
    return totals[0], parts


def send_parts(parts, term_count):
    sent = [
        along_term(parts[i - 1], lambda t, b=i: t ^ (2 * b), term_count)
        for i in range(len(parts), 0, -1)
    ]
    return sent[::-1]


def everyones(tile, count):
    return lax.all_to_all(jnp.broadcast_to(tile, (count,) + tile.shape), ("sec", "term"), 0, 0)


def lane_sums(tile, products):
    for k, (a, b) in products.items():
        line = jnp.sum(a * b, axis=0, keepdims=True)
        tile[k : k + 1, :] = sum(line[:, j : j + 128] for j in range(0, line.shape[1], 128))


def image_kernel(x_ref, own, *refs):
    y_ref, shard, tile = refs[-3:]
    y = own[...]
    for part in refs[:-3]:
        y = y + part[...].astype(jnp.float32)
    y = y * SCALE
    y_ref[...] = y
    shard[0] = y.astype(jnp.bfloat16)
    x = x_ref[0].astype(jnp.float32)
    tile[...] = jnp.zeros_like(tile)
    lane_sums(tile, {0: (x, x), 1: (x, y), 2: (y, y)})


def gram_kernel(before, x_ref, y_ref, own, *refs):
    h_ref, tile = refs[-2:]
    h = own[...]
    for part in refs[:-2]:
        h = h + part[...].astype(jnp.float32)
    h_ref[...] = h
    x, y = x_ref[0].astype(jnp.float32), y_ref[...]
    tile[...] = before[...]
    lane_sums(tile, {3: (x, h), 4: (y, h), 5: (h, h)})


def finish_kernel(tiles, x_ref, y_ref, h_ref, vector, alphas, betas):
    sums = jnp.sum(jnp.sum(tiles[...], axis=0), axis=1, keepdims=True)
    xx, xy, yy, xh, yh, hh = (sums[k : k + 1, :] for k in range(6))
    cx = 1.0 / jnp.sqrt(xx + EPS)
    cy = cx / SCALE
    vv, vi, ii = xx * cx * cx, xy * cx * cy, yy * cy * cy
    vh, ih, hh = xh * cx * cy, yh * cy * cy, hh * cy * cy
    alpha0 = vi
    square0 = ii - 2.0 * alpha0 * vi + alpha0 * alpha0 * vv
    beta0 = jnp.sqrt(jnp.maximum(square0, 0.0) + EPS)
    inv = 1.0 / beta0
    ui = (ii - alpha0 * vi) * inv
    uh = (ih - alpha0 * vh) * inv
    uv = (vi - alpha0 * vv) * inv
    uu = (ui - alpha0 * uv) * inv
    jv = (vh - alpha0 * vi) * inv
    jj = (hh - 2.0 * alpha0 * ih + alpha0 * alpha0 * ii) * inv * inv
    alpha1 = (uh - alpha0 * ui) * inv
    square1 = (
        jj + alpha1 * alpha1 * uu + beta0 * beta0 * vv
        - 2.0 * alpha1 * alpha1 - 2.0 * beta0 * jv + 2.0 * alpha1 * beta0 * uv
    )
    beta1 = jnp.sqrt(jnp.maximum(square1, 0.0) + EPS)
    last = 1.0 / beta1
    ch = inv * last * cy
    ci = -(alpha0 + alpha1) * inv * last * cy
    cv = (alpha1 * alpha0 * inv - beta0) * last * cx
    vector[0] = ch * h_ref[...] + ci * y_ref[...] + cv * x_ref[0].astype(jnp.float32)
    alphas[0], alphas[1] = alpha0[0, 0], alpha1[0, 0]
    betas[0], betas[1] = beta0[0, 0], beta1[0, 0]


def on_device(theta, left_env, right_env, term_shift, term_on, block_rows, block_cols):
    rows, width = theta.shape[1:]
    terms = left_env.shape[0]
    sec_count, term_count = lax.axis_size("sec"), lax.axis_size("term")
    sec, term = lax.axis_index("sec"), lax.axis_index("term")
    row = term * rows + lax.broadcasted_iota(jnp.int32, (1, rows, width), 1)
    col = lax.broadcasted_iota(jnp.int32, (1, rows, width), 2)
    start = jnp.where((row < block_rows[0]) & (col < block_cols[0]), theta, jnp.zeros_like(theta))
    toward_pair = 1 - 2 * (sec % 2)
    source = jnp.where(term_shift == 0, 0, jnp.where(term_shift == toward_pair, 1, 2))
    scal = jnp.concatenate(
        [source, term_on[:, 0], jnp.stack([term // 2, term % 2]), block_rows, block_cols]
    ).astype(jnp.int32)

    vmem, smem = (pl.BlockSpec(memory_space=m) for m in (pltpu.VMEM, pltpu.SMEM))
    small = pltpu.CompilerParams(vmem_limit_bytes=8 * 2**20)
    block = jax.ShapeDtypeStruct((rows, width), jnp.float32)
    tile = jax.ShapeDtypeStruct((8, 128), jnp.float32)
    pair = jax.ShapeDtypeStruct((2,), jnp.float32)

    pieces, scal = gather_pieces(start, scal, FIRST, sec_count, term_count)
    mine, theirs = apply_terms(scal, left_env, right_env, pieces, FIRST, rows)
    own, got = reduce_parts(mine, theirs, term_count)
    local = lax.optimization_barrier((left_env, right_env, own))[:2]
    swapped = [along_term(a, lambda t: t ^ 1, term_count) for a in local]
    table = along_term(lax.optimization_barrier((scal[: 2 * terms], pieces[3]))[0], lambda t: t ^ 1, term_count)
    own, swapped = lax.optimization_barrier((own, swapped))
    envs = (left_env, swapped[0], right_env, swapped[1])
    y, shard, sums = pl.pallas_call(
        image_kernel,
        out_shape=(block, jax.ShapeDtypeStruct((1, rows, width), jnp.bfloat16), tile),
        in_specs=[vmem] * (2 + len(got)),
        out_specs=(vmem,) * 3,
        compiler_params=small,
        name="image",
    )(start, own, *got)
    pieces, _ = gather_pieces(shard, (), SECOND, sec_count, term_count)
    own, parts = apply_chip_terms(scal, table, envs, pieces, SECOND, rows)
    got = send_parts(parts, term_count)
    h, sums = pl.pallas_call(
        gram_kernel,
        out_shape=(block, tile),
        in_specs=[vmem] * (4 + len(got)),
        out_specs=(vmem, vmem),
        compiler_params=small,
        name="gram",
    )(sums, start, y, own, *got[1:], got[0])
    sums = everyones(sums, sec_count * term_count)
    vector, alphas, betas = pl.pallas_call(
        finish_kernel,
        out_shape=(jax.ShapeDtypeStruct((1, rows, width), jnp.float32), pair, pair),
        in_specs=[vmem] * 4,
        out_specs=(vmem, smem, smem),
        compiler_params=small,
        name="finish",
    )(sums, start, y, h)
    return (vector, alphas, betas)


def solution(mesh):
    return jax.shard_map(
        on_device,
        mesh=mesh,
        in_specs=(
            P("sec", "term", None),
            P("term", "sec", None, None),
            P("term", "sec", None, None),
            P("term"),
            P("term", "sec"),
            P("sec"),
            P("sec"),
        ),
        out_specs=(P("sec", "term", None), P(), P()),
        check_vma=False,
    )
```
